32 devices in a mesh: mem: 8 (over y, x, core), lat: 4 (over z).
Axes of the slice: x: 2, y: 2, z: 4, core: 2. Of those that a mesh axis runs over, the one named last changes fastest.
Arguments:
- fields: float32 [1024, 32, 256], P('mem', 'lat'), may hold values from -8 to 8
- forcing: float32 [32, 256], P('lat'), may hold values from 2 to 8
- obs_cell: int32 [4, 32, 256], P('lat'), may hold values from 0 to 63
- obs_count: int32 [4, 32], P('lat', 'mem'), may hold values from 64 to 256, as said below
- obs_value: float32 [4, 32, 256], P('lat', 'mem'), may hold values from -12 to 12
- obs_var: float32 [4, 32, 256], P('lat', 'mem'), may hold values from 0.25 to 1
Outputs:
- analysis: float32 [1024, 32, 256], P('mem', 'lat')
The draws below stay inside these ranges and needn't reach their ends.
Inputs may be any that keep to these rules, and one draw needn't show every extreme that they name: `obs_count`: each latitude strip has a patch with exactly 256 live observations.
All inputs are finite; a program needn't handle non-finite values.
Results may differ from the reference program's by a relative error of at most 0.0003.
Values sent between devices are 32-bit elements; how exact they have to be, the bound alone decides.
A program may use at most 64 MiB of HBM per device.

```python
import math
import jax
import jax.numpy as jnp
from jax import lax

MEMBERS = 1024
OBS = 256
PATCH_CELLS = 64
NLON = 256
STEPS = 4
NROWS = 32
PATCHES_STRIP = 32
N_LAT = 4


def draw_obs_count(key, part):
    first_key = jax.random.fold_in(key, 11)
    second_key = jax.random.fold_in(key, 23)
    drawn = jax.random.randint(first_key, (N_LAT, PATCHES_STRIP), OBS // 4, OBS + 1)
    chosen_slot = jax.random.randint(second_key, (N_LAT, 1), 0, PATCHES_STRIP)
    picked = jnp.arange(PATCHES_STRIP)[None, :] == chosen_slot
    return jnp.where(picked, OBS, drawn).astype(jnp.int32)


def touch_ends(values, key, smallest, top_value):
    index_at = [jax.random.randint(jax.random.fold_in(key, axis), (), 0, length) for axis, length in enumerate(values.shape)]
    widest = values.shape.index(max(values.shape))
    beside = index_at[:widest] + [(index_at[widest] + 1) % values.shape[widest]] + index_at[widest + 1:]
    return values.at[tuple(index_at)].set(smallest).at[tuple(beside)].set(top_value)


def block_scale(own_key, dims, cuts, smallest, largest):
    gain, own = 1.0, jax.random.fold_in(own_key, 6)
    for position, parts in cuts:
        draws = jnp.exp(jax.random.uniform(jax.random.fold_in(own, position), (parts,), jnp.float32, smallest / len(cuts), largest / len(cuts)))
        gain = gain * jnp.repeat(draws, dims[position] // parts).reshape([-1 if axis == position else 1 for axis in range(len(dims))])
    return gain


def bell_draw(own_key, extent, scale, limit, cuts=(), dtype=jnp.bfloat16):
    entries = scale * jax.random.normal(own_key, extent, jnp.float32)
    if cuts:
        entries = entries * block_scale(own_key, extent, cuts, -0.22, 0.18)
    return jnp.clip(entries, -limit, limit).astype(dtype)


def setup_inputs(seed: int = 0) -> dict:
    key_of = jax.random.split(jax.random.key(seed), 7)
    return {
        "fields": bell_draw(key_of[0], (MEMBERS, NROWS, NLON), 2.0, 8.0, ((0, 8), (1, 4)), jnp.float32),
        "forcing": jnp.clip(2.0 + 6.0 * jax.random.uniform(key_of[1], (NROWS, NLON), jnp.float32) ** block_scale(key_of[1], (NROWS, NLON), ((0, 4),), -0.2, 0.2), 2.0, 8.0),
        "obs_cell": touch_ends(jax.random.randint(key_of[2], (N_LAT, PATCHES_STRIP, OBS), 0, PATCH_CELLS), jax.random.fold_in(key_of[2], 1), 0, PATCH_CELLS - 1).astype(jnp.int32),
        "obs_count": draw_obs_count(jax.random.fold_in(key_of[6], 71), 0),
        "obs_value": bell_draw(key_of[4], (N_LAT, PATCHES_STRIP, OBS), 3.0, 12.0, ((0, 4), (1, 8)), jnp.float32),
        "obs_var": jnp.clip(jnp.exp(math.log(1.0) - 1.3862944 * jax.random.uniform(key_of[5], (N_LAT, PATCHES_STRIP, OBS), jnp.float32) ** block_scale(key_of[5], (N_LAT, PATCHES_STRIP, OBS), ((0, 4), (1, 8)), -0.2, 0.2)), 0.25, 1.0),
    }


TIME_STEP = 0.05
LAT_MIXING = 4.0

def advance(middle, upper, lower, forcing):
    eastern = jnp.roll(middle, -1, axis=2)
    western = jnp.roll(middle, 1, axis=2)
    far_west = jnp.roll(middle, 2, axis=2)
    tendency = (eastern - far_west) * western - middle + forcing + LAT_MIXING * (upper + lower - 2.0 * middle)
    return middle + TIME_STEP * tendency

def analyse(patch_cells, observed, live_count, values, variances):
    members = patch_cells.shape[1]
    anomalies = patch_cells - jnp.mean(patch_cells, axis=1, keepdims=True)
    mean_obs = jnp.mean(observed, axis=1, keepdims=True)
    live = (jnp.arange(observed.shape[0]).astype(jnp.int32) < live_count)[:, None]
    obs_anom = jnp.where(live, observed - mean_obs, jnp.float32(0.0))
    gram = jnp.dot(obs_anom, obs_anom.T, precision=lax.Precision.HIGHEST) / (members - 1)
    gram = gram + jnp.diag(jnp.where(live[:, 0], variances, jnp.float32(1.0)))
    innovation = jnp.where(live, values[:, None] - mean_obs, jnp.float32(0.0))
    target = innovation - 0.5 * obs_anom
    factor = jnp.linalg.cholesky(gram)
    solved = jax.scipy.linalg.cho_solve((factor, True), target)
    cross = jnp.dot(anomalies, obs_anom.T, precision=lax.Precision.HIGHEST) / (members - 1)
    return patch_cells + jnp.dot(cross, solved, precision=lax.Precision.HIGHEST)

def reference(fields, forcing, obs_cell, obs_count, obs_value, obs_var):
    current = fields
    for repeat_index in range(STEPS):
        padded = jnp.pad(current, ((0, 0), (1, 1), (0, 0)))
        current = advance(current, padded[:, 2:], padded[:, :-2], forcing)
    members = current.shape[0]
    total_patches = N_LAT * PATCHES_STRIP
    patches = current.reshape(members, total_patches, PATCH_CELLS).transpose(1, 2, 0)

    def one_patch(items):
        patch_cells, cell_index, live_count, values, variances = items
        observed = jnp.take(patch_cells, cell_index, axis=0)
        return analyse(patch_cells, observed, live_count, values, variances)
    result = lax.map(one_patch, (patches, obs_cell.reshape(total_patches, OBS), obs_count.reshape(total_patches), obs_value.reshape(total_patches, OBS), obs_var.reshape(total_patches, OBS)))
    return result.transpose(2, 0, 1).reshape(members, NROWS, NLON)
```

```python
import functools

import jax
import jax.numpy as jnp
from jax import lax
from jax.experimental import pallas as pl
from jax.experimental.pallas import tpu as pltpu
from jax.sharding import PartitionSpec as P

PATCH_CELLS = 64
STEPS = 4
TIME_STEP = 0.05
LAT_MIXING = 4.0
HALO_CHUNKS = 4
TILE = 8

MESH = pl.DeviceIdType.MESH
HIGHEST = lax.Precision.HIGHEST


def lane_group(shape):
    return lax.broadcasted_iota(jnp.int32, shape, 1) // PATCH_CELLS


def diagonal_blocks(square):
    lon = square.shape[1]
    groups = lane_group((PATCH_CELLS, lon))
    total = jnp.zeros((PATCH_CELLS, lon), jnp.float32)
    for q in range(lon // PATCH_CELLS):
        block = square[q * PATCH_CELLS:(q + 1) * PATCH_CELLS]
        total = jnp.where(groups == q, block, total)
    return total


def block_diagonal(blocks):
    lon = blocks.shape[1]
    groups = lane_group(blocks.shape)
    return jnp.concatenate(
        [jnp.where(groups == q, blocks, 0.0) for q in range(lon // PATCH_CELLS)], axis=0
    )


def as_column(row, eye, groups):
    spread = jnp.where(eye, jnp.broadcast_to(row, eye.shape), 0.0)
    total = jnp.zeros(eye.shape, jnp.float32)
    for q in range(eye.shape[1] // PATCH_CELLS):
        column = jnp.sum(jnp.where(groups == q, spread, 0.0), axis=1, keepdims=True)
        total = jnp.where(groups == q, column, total)
    return total


def invert(blocks, in_group):
    lon = blocks.shape[1]
    sublane = lax.broadcasted_iota(jnp.int32, (PATCH_CELLS, 128), 0)
    lane = lax.broadcasted_iota(jnp.int32, (PATCH_CELLS, 128), 1)
    start = (lane // PATCH_CELLS) * PATCH_CELLS
    position = lane - start
    halves = [blocks[:, h * 128:(h + 1) * 128] for h in range(lon // 128)]
    for k in range(PATCH_CELLS):
        at_k = position == k
        on_row = sublane == k
        source = start + k
        updated = []
        for half in halves:
            column = jnp.take_along_axis(half, source, axis=1, mode="promise_in_bounds")
            inverse = 1.0 / column[k:k + 1]
            row = jnp.where(at_k[k:k + 1], 1.0, half[k:k + 1]) * inverse
            base = jnp.where(at_k | on_row, 0.0, half)
            factor = jnp.where(on_row, -1.0, column)
            updated.append(base - factor * row)
        halves = updated
    return jnp.concatenate(halves, axis=1)


def kernel(n_mem, n_lat, fields_ref, forcing_ref, cell_ref, count_ref, value_ref, var_ref, out_ref,
           ext, cur, fbuf, fwide, gsend, grecv, nsend, nrecv,
           halo_send, halo_recv, force_send, force_recv, gram_send, gram_recv, gain_send, gain_recv):
    rows, members, lon = cur.shape
    share = n_mem // rows
    per_row = lon // PATCH_CELLS
    chunk = members // HALO_CHUNKS
    me = lax.axis_index("mem")
    strip = lax.axis_index("lat")
    has_before = strip > 0
    has_after = strip < n_lat - 1
    my_row = me // share
    solver = lax.rem(me, share) == 0

    barrier = pltpu.get_barrier_semaphore()
    for d in range(1, n_mem):
        pl.semaphore_signal(barrier, inc=1, device_id={"mem": lax.rem(me + d, n_mem)}, device_id_type=MESH)

    @pl.when(has_before)
    def _():
        pl.semaphore_signal(barrier, inc=1, device_id={"lat": strip - 1}, device_id_type=MESH)

    @pl.when(has_after)
    def _():
        pl.semaphore_signal(barrier, inc=1, device_id={"lat": strip + 1}, device_id_type=MESH)

    for r in range(rows):
        for h in range(lon // 128):
            ext[STEPS + r, :, h * 128:(h + 1) * 128] = fields_ref[
                pl.ds(h * rows + r, members, stride=rows * (lon // 128)), :]

    @pl.when(jnp.logical_not(has_before))
    def _():
        ext[0:STEPS] = jnp.zeros((STEPS, members, lon), jnp.float32)
        fbuf[0] = jnp.zeros((rows, lon), jnp.float32)

    @pl.when(jnp.logical_not(has_after))
    def _():
        ext[STEPS + rows:] = jnp.zeros((STEPS, members, lon), jnp.float32)
        fbuf[1] = jnp.zeros((rows, lon), jnp.float32)

    pl.semaphore_wait(barrier, n_mem - 1 + has_before.astype(jnp.int32) + has_after.astype(jnp.int32))

    def halo_copy(side, c):
        span = pl.ds(c * chunk, chunk)
        source, target = ((rows, 0), (STEPS, STEPS + rows))[side]
        return pltpu.make_async_remote_copy(
            src_ref=ext.at[pl.ds(source, STEPS), span],
            dst_ref=ext.at[pl.ds(target, STEPS), span],
            send_sem=halo_send.at[side, c],
            recv_sem=halo_recv.at[side, c],
            device_id={"lat": (strip + 1, strip - 1)[side]},
            device_id_type=MESH,
        )

    def force_copy(side):
        return pltpu.make_async_remote_copy(
            src_ref=forcing_ref,
            dst_ref=fbuf.at[side],
            send_sem=force_send.at[side],
            recv_sem=force_recv.at[side],
            device_id={"lat": (strip + 1, strip - 1)[side]},
            device_id_type=MESH,
        )

    can_send = (has_after, has_before)
    can_receive = (has_before, has_after)
    for side in range(2):
        @pl.when(can_send[side])
        def _(side=side):
            force_copy(side).start()
    for c in range(HALO_CHUNKS):
        for side in range(2):
            @pl.when(can_send[side])
            def _(side=side, c=c):
                halo_copy(side, c).start()

    cell_of = lax.broadcasted_iota(jnp.int32, (PATCH_CELLS, cell_ref.shape[1]), 0)
    slot = lax.broadcasted_iota(jnp.int32, (1, cell_ref.shape[1]), 1)
    groups = lane_group((PATCH_CELLS, lon))
    weight = jnp.zeros((PATCH_CELLS, lon), jnp.float32)
    pull = jnp.zeros((PATCH_CELLS, lon), jnp.float32)
    for q in range(per_row):
        cells = cell_ref[pl.ds(my_row * per_row + q, 1), :]
        precision = jnp.where(slot < count_ref[0, q], 1.0 / var_ref[q:q + 1, :], 0.0)
        hit = cell_of == cells
        w = jnp.sum(jnp.where(hit, precision, 0.0), axis=1, keepdims=True)
        b = jnp.sum(jnp.where(hit, precision * value_ref[q:q + 1, :], 0.0), axis=1, keepdims=True)
        weight = jnp.where(groups == q, w, weight)
        pull = jnp.where(groups == q, b, pull)

    for side in range(2):
        @pl.when(can_receive[side])
        def _(side=side):
            force_copy(side).wait_recv()
    own = forcing_ref[...]
    for i in range(2 * STEPS + rows):
        if i < STEPS:
            line = fbuf[0, rows - STEPS + i:rows - STEPS + i + 1, :]
        elif i < STEPS + rows:
            line = own[i - STEPS:i - STEPS + 1]
        else:
            line = fbuf[1, i - STEPS - rows:i - STEPS - rows + 1, :]
        fwide[i] = jnp.broadcast_to(line * TIME_STEP, (TILE, lon))

    def advance(u, upper, lower, force):
        eastern = pltpu.roll(u, lon - 1, 1)
        western = pltpu.roll(u, 1, 1)
        far_west = pltpu.roll(u, 2, 1)
        tendency = (eastern - far_west) * western - u + LAT_MIXING * (upper + lower - 2.0 * u)
        return u + (TIME_STEP * tendency + force)

    def forecast(start):
        span = pl.ds(pl.multiple_of(start, TILE), TILE)
        state = [ext[i, span, :] for i in range(2 * STEPS + rows)]
        for step in range(STEPS):
            lo = step + 1
            fresh = []
            for i in range(lo, 2 * STEPS + rows - lo):
                at = i - step
                moved = advance(state[at], state[at + 1], state[at - 1], fwide[i])
                if i < STEPS:
                    moved = jnp.where(has_before, moved, 0.0)
                elif i >= STEPS + rows:
                    moved = jnp.where(has_after, moved, 0.0)
                fresh.append(moved)
            state = fresh
        for r in range(rows):
            cur[r, span, :] = state[r]

    for c in range(HALO_CHUNKS):
        for side in range(2):
            @pl.when(can_receive[side])
            def _(side=side, c=c):
                halo_copy(side, c).wait_recv()

        @pl.loop(0, chunk // TILE)
        def _(i, c=c):
            forecast(c * chunk + i * TILE)

    def gram_copy(d):
        target = lax.rem(me + d, n_mem)
        return pltpu.make_async_remote_copy(
            src_ref=gsend.at[target // share],
            dst_ref=grecv.at[d - 1],
            send_sem=gram_send.at[d - 1],
            recv_sem=gram_recv.at[d - 1],
            device_id={"mem": target},
            device_id_type=MESH,
        )

    def moments(row):
        values = cur[row]
        mean = jnp.sum(values, axis=0, keepdims=True) * (1.0 / members)
        centred = values - mean
        square = lax.dot_general(
            centred, centred, (((0,), (0,)), ((), ())), precision=HIGHEST,
            preferred_element_type=jnp.float32,
        )
        gsend[row, 0:PATCH_CELLS, :] = diagonal_blocks(square)
        gsend[row, PATCH_CELLS:, :] = jnp.broadcast_to(mean, (TILE, lon))

    @pl.loop(1, n_mem)
    def _(d):
        target = lax.rem(me + d, n_mem)

        @pl.when(lax.rem(target, share) == 0)
        def _():
            moments(target // share)
            gram_copy(d).start()

    def gain_copy(d):
        return pltpu.make_async_remote_copy(
            src_ref=nsend,
            dst_ref=nrecv.at[my_row],
            send_sem=gain_send.at[d - 1],
            recv_sem=gain_recv.at[d - 1],
            device_id={"mem": lax.rem(me + d, n_mem)},
            device_id_type=MESH,
        )

    def apply(row, gain_ref):
        mean = gain_ref[PATCH_CELLS:PATCH_CELLS + 1, :]
        shift = gain_ref[PATCH_CELLS + 1:PATCH_CELLS + 2, :]
        half = 0.5 * (cur[row] - mean)
        moved = jnp.dot(half, block_diagonal(gain_ref[0:PATCH_CELLS, :]), precision=HIGHEST,
                        preferred_element_type=jnp.float32)
        result = half + moved + (mean + shift)
        for h in range(lon // 128):
            out_ref[pl.ds(h * rows + row, members, stride=rows * (lon // 128)), :] = result[:, h * 128:(h + 1) * 128]

    @pl.when(solver)
    def _():
        moments(my_row)
        total = gsend[my_row, 0:PATCH_CELLS, :]
        means = [gsend[my_row, PATCH_CELLS:, :]]
        for d in range(1, n_mem):
            gram_copy(d).wait_recv()
            total = total + grecv[d - 1, 0:PATCH_CELLS, :]
            means.append(grecv[d - 1, PATCH_CELLS:, :])
        mean = functools.reduce(lambda a, b: a + b, means)[0:1] * (1.0 / n_mem)
        drift = jnp.concatenate([m[0:1] - mean for m in means], axis=0)
        spread = lax.dot_general(
            drift, drift, (((0,), (0,)), ((), ())), precision=HIGHEST, preferred_element_type=jnp.float32
        )
        cov = (total + members * diagonal_blocks(spread)) * (1.0 / (members * n_mem - 1))

        in_group = lax.broadcasted_iota(jnp.int32, (PATCH_CELLS, lon), 1) - groups * PATCH_CELLS
        eye = lax.broadcasted_iota(jnp.int32, (PATCH_CELLS, lon), 0) == in_group
        inverse = invert(jnp.where(eye, 1.0, 0.0) + weight * cov, in_group)
        misfit = pull - weight * as_column(mean, eye, groups)
        push = jnp.sum(misfit * cov, axis=0, keepdims=True)
        shift = jnp.sum(as_column(push, eye, groups) * inverse, axis=0, keepdims=True)
        nsend[0:PATCH_CELLS, :] = inverse
        first = lax.broadcasted_iota(jnp.int32, (TILE, lon), 0) == 0
        nsend[PATCH_CELLS:, :] = jnp.where(first, mean, shift)
        for d in range(1, n_mem):
            gain_copy(d).start()
        apply(my_row, nsend)

    @pl.loop(1, n_mem)
    def _(d):
        origin = lax.rem(me + n_mem - d, n_mem)

        @pl.when(lax.rem(origin, share) == 0)
        def _():
            gain_copy(d).wait_recv()
            apply(origin // share, nrecv.at[origin // share])

    for side in range(2):
        @pl.when(can_send[side])
        def _(side=side):
            force_copy(side).wait_send()
            for c in range(HALO_CHUNKS):
                halo_copy(side, c).wait_send()

    @pl.loop(1, n_mem)
    def _(d):
        @pl.when(lax.rem(lax.rem(me + d, n_mem), share) == 0)
        def _():
            gram_copy(d).wait_send()

        @pl.when(solver)
        def _():
            gain_copy(d).wait_send()


def local(n_mem, n_lat, fields, forcing, obs_cell, obs_count, obs_value, obs_var):
    members, rows, lon = fields.shape
    slots = obs_cell.shape[2]
    per_row = lon // PATCH_CELLS
    if obs_count.shape[1] != per_row:
        row = lax.axis_index("mem") // (n_mem // rows)
        obs_count, obs_value, obs_var = (
            lax.dynamic_slice_in_dim(lax.all_gather(a, "mem", axis=1, tiled=True), row * per_row, per_row, 1)
            for a in (obs_count, obs_value, obs_var)
        )
    block = PATCH_CELLS + TILE
    vmem = pl.BlockSpec(memory_space=pltpu.VMEM)
    dma = pltpu.SemaphoreType.DMA
    out = pl.pallas_call(
        functools.partial(kernel, n_mem, n_lat),
        out_shape=jax.ShapeDtypeStruct((members * rows * (lon // 128), 128), jnp.float32),
        in_specs=[vmem, vmem, vmem, pl.BlockSpec(memory_space=pltpu.SMEM), vmem, vmem],
        out_specs=vmem,
        scratch_shapes=[
            pltpu.VMEM((rows + 2 * STEPS, members, lon), jnp.float32),
            pltpu.VMEM((rows, members, lon), jnp.float32),
            pltpu.VMEM((2, rows, lon), jnp.float32),
            pltpu.VMEM((rows + 2 * STEPS, TILE, lon), jnp.float32),
            pltpu.VMEM((rows, block, lon), jnp.float32),
            pltpu.VMEM((n_mem - 1, block, lon), jnp.float32),
            pltpu.VMEM((block, lon), jnp.float32),
            pltpu.VMEM((rows, block, lon), jnp.float32),
            dma((2, HALO_CHUNKS)), dma((2, HALO_CHUNKS)),
            dma((2,)), dma((2,)),
            dma((n_mem - 1,)), dma((n_mem - 1,)),
            dma((n_mem - 1,)), dma((n_mem - 1,)),
        ],
        compiler_params=pltpu.CompilerParams(collective_id=0, has_side_effects=True),
        name="cycle",
    )(
        fields.reshape(members, rows, lon // 128, 128).transpose(0, 2, 1, 3).reshape(-1, 128),
        forcing,
        obs_cell.reshape(-1, slots),
        obs_count,
        obs_value.reshape(-1, slots),
        obs_var.reshape(-1, slots),
    )
    return out.reshape(members, lon // 128, rows, 128).transpose(0, 2, 1, 3).reshape(members, rows, lon)


def solution(mesh):
    placed = (
        P("mem", "lat", None),
        P("lat", None),
        P("lat", None, None),
        P("lat", "mem"),
        P("lat", "mem", None),
        P("lat", "mem", None),
    )
    return jax.shard_map(
        functools.partial(local, mesh.shape["mem"], mesh.shape["lat"]),
        mesh=mesh, in_specs=placed, out_specs=P("mem", "lat", None), check_vma=False,
    )
```

```python
import functools

import jax
import jax.numpy as jnp
from jax import lax
from jax.experimental import pallas as pl
from jax.experimental.pallas import tpu as pltpu
from jax.sharding import PartitionSpec as P

PATCH_CELLS = 64
STEPS = 4
TIME_STEP = 0.05
LAT_MIXING = 4.0
HALO_CHUNKS = 4
TILE = 8
PIVOTS = 4

MESH = pl.DeviceIdType.MESH
HIGHEST = lax.Precision.HIGHEST


def lane_group(shape):
    return lax.broadcasted_iota(jnp.int32, shape, 1) // PATCH_CELLS


def diagonal_blocks(square):
    lon = square.shape[1]
    groups = lane_group((PATCH_CELLS, lon))
    total = jnp.zeros((PATCH_CELLS, lon), jnp.float32)
    for q in range(lon // PATCH_CELLS):
        block = square[q * PATCH_CELLS:(q + 1) * PATCH_CELLS]
        total = jnp.where(groups == q, block, total)
    return total


def block_diagonal(blocks):
    lon = blocks.shape[1]
    groups = lane_group(blocks.shape)
    return jnp.concatenate(
        [jnp.where(groups == q, blocks, 0.0) for q in range(lon // PATCH_CELLS)], axis=0
    )


def as_column(row, eye, groups):
    spread = jnp.where(eye, jnp.broadcast_to(row, eye.shape), 0.0)
    total = jnp.zeros(eye.shape, jnp.float32)
    for q in range(eye.shape[1] // PATCH_CELLS):
        column = jnp.sum(jnp.where(groups == q, spread, 0.0), axis=1, keepdims=True)
        total = jnp.where(groups == q, column, total)
    return total


def invert(blocks):
    lon = blocks.shape[1]
    sublane = lax.broadcasted_iota(jnp.int32, (PATCH_CELLS, 128), 0)
    lane = lax.broadcasted_iota(jnp.int32, (PATCH_CELLS, 128), 1)
    start = (lane // PATCH_CELLS) * PATCH_CELLS
    position = lane - start
    halves = [blocks[:, h * 128:(h + 1) * 128] for h in range(lon // 128)]
    span = range(PIVOTS)
    for k in range(0, PATCH_CELLS, PIVOTS):
        in_columns = (position >= k) & (position < k + PIVOTS)
        in_rows = (sublane >= k) & (sublane < k + PIVOTS)
        updated = []
        for half in halves:
            columns = [
                jnp.take_along_axis(half, start + (k + j), axis=1, mode="promise_in_bounds") for j in span
            ]
            small = [[columns[j][k + i:k + i + 1] for j in span] for i in span]
            rows = [
                jnp.where(
                    in_columns[0:1],
                    jnp.where(position[0:1] == k + i, 1.0, 0.0),
                    half[k + i:k + i + 1],
                )
                for i in span
            ]
            for i in span:
                inverse = 1.0 / small[i][i]
                rows[i] = rows[i] * inverse
                for j in range(i + 1, PIVOTS):
                    small[i][j] = small[i][j] * inverse
                for other in span:
                    if other != i:
                        factor = small[other][i]
                        rows[other] = rows[other] - factor * rows[i]
                        for j in range(i + 1, PIVOTS):
                            small[other][j] = small[other][j] - factor * small[i][j]
            fresh = jnp.where(in_columns | in_rows, 0.0, half)
            for j in span:
                factor = jnp.where(in_rows, jnp.where(sublane == k + j, -1.0, 0.0), columns[j])
                fresh = fresh - factor * rows[j]
            updated.append(fresh)
        halves = updated
    return jnp.concatenate(halves, axis=1)


def split(values):
    high = values.astype(jnp.bfloat16)
    return high, (values - high.astype(jnp.float32)).astype(jnp.bfloat16)


def kernel(n_mem, n_lat, fields_ref, forcing_ref, cell_ref, count_ref, value_ref, var_ref, out_ref,
           landed, ext, cur, fbuf, fwide, gsend, grecv, nsend, nrecv,
           load_sem, halo_send, halo_recv, force_send, force_recv, gram_send, gram_recv, gain_send, gain_recv):
    rows, members, lon = cur.shape
    share = n_mem // rows
    per_row = lon // PATCH_CELLS
    chunk = members // HALO_CHUNKS
    me = lax.axis_index("mem")
    strip = lax.axis_index("lat")
    has_before = strip > 0
    has_after = strip < n_lat - 1
    my_row = me // share
    solver = lax.rem(me, share) == 0

    barrier = pltpu.get_barrier_semaphore()
    for d in range(1, n_mem):
        pl.semaphore_signal(barrier, inc=1, device_id={"mem": lax.rem(me + d, n_mem)}, device_id_type=MESH)

    @pl.when(has_before)
    def _():
        pl.semaphore_signal(barrier, inc=1, device_id={"lat": strip - 1}, device_id_type=MESH)

    @pl.when(has_after)
    def _():
        pl.semaphore_signal(barrier, inc=1, device_id={"lat": strip + 1}, device_id_type=MESH)

    pitch = rows * (lon // 128)

    def load(c):
        span = pl.ds(c * chunk * pitch, chunk * pitch)
        return pltpu.make_async_copy(fields_ref.at[span], landed.at[span], load_sem.at[c])

    for c in range(HALO_CHUNKS):
        load(c).start()

    def rows_first(c):
        load(c).wait()
        for r in range(rows):
            for h in range(lon // 128):
                ext[STEPS + r, c * chunk:(c + 1) * chunk, h * 128:(h + 1) * 128] = landed[
                    pl.ds(c * chunk * pitch + h * rows + r, chunk, stride=pitch), :]

    rows_first(0)
    pl.semaphore_wait(barrier, n_mem - 1 + has_before.astype(jnp.int32) + has_after.astype(jnp.int32))

    def halo_copy(side, c):
        span = pl.ds(c * chunk, chunk)
        source, target = ((rows, 0), (STEPS, STEPS + rows))[side]
        return pltpu.make_async_remote_copy(
            src_ref=ext.at[pl.ds(source, STEPS), span],
            dst_ref=ext.at[pl.ds(target, STEPS), span],
            send_sem=halo_send.at[side, c],
            recv_sem=halo_recv.at[side, c],
            device_id={"lat": (strip + 1, strip - 1)[side]},
            device_id_type=MESH,
        )

    def force_copy(side):
        return pltpu.make_async_remote_copy(
            src_ref=forcing_ref,
            dst_ref=fbuf.at[side],
            send_sem=force_send.at[side],
            recv_sem=force_recv.at[side],
            device_id={"lat": (strip + 1, strip - 1)[side]},
            device_id_type=MESH,
        )

    can_send = (has_after, has_before)
    can_receive = (has_before, has_after)
    for side in range(2):
        @pl.when(can_send[side])
        def _(side=side):
            force_copy(side).start()
    for c in range(HALO_CHUNKS):
        if c:
            rows_first(c)
        for side in range(2):
            @pl.when(can_send[side])
            def _(side=side, c=c):
                halo_copy(side, c).start()

    @pl.when(jnp.logical_not(has_before))
    def _():
        ext[0:STEPS] = jnp.zeros((STEPS, members, lon), jnp.float32)
        fbuf[0] = jnp.zeros((rows, lon), jnp.float32)

    @pl.when(jnp.logical_not(has_after))
    def _():
        ext[STEPS + rows:] = jnp.zeros((STEPS, members, lon), jnp.float32)
        fbuf[1] = jnp.zeros((rows, lon), jnp.float32)

    cell_of = lax.broadcasted_iota(jnp.int32, (PATCH_CELLS, cell_ref.shape[1]), 0)
    slot = lax.broadcasted_iota(jnp.int32, (1, cell_ref.shape[1]), 1)
    groups = lane_group((PATCH_CELLS, lon))
    weight = jnp.zeros((PATCH_CELLS, lon), jnp.float32)
    pull = jnp.zeros((PATCH_CELLS, lon), jnp.float32)
    for q in range(per_row):
        cells = cell_ref[pl.ds(my_row * per_row + q, 1), :]
        precision = jnp.where(slot < count_ref[0, q], 1.0 / var_ref[q:q + 1, :], 0.0)
        hit = cell_of == cells
        w = jnp.sum(jnp.where(hit, precision, 0.0), axis=1, keepdims=True)
        b = jnp.sum(jnp.where(hit, precision * value_ref[q:q + 1, :], 0.0), axis=1, keepdims=True)
        weight = jnp.where(groups == q, w, weight)
        pull = jnp.where(groups == q, b, pull)

    for side in range(2):
        @pl.when(can_receive[side])
        def _(side=side):
            force_copy(side).wait_recv()
    own = forcing_ref[...]
    for i in range(2 * STEPS + rows):
        if i < STEPS:
            line = fbuf[0, rows - STEPS + i:rows - STEPS + i + 1, :]
        elif i < STEPS + rows:
            line = own[i - STEPS:i - STEPS + 1]
        else:
            line = fbuf[1, i - STEPS - rows:i - STEPS - rows + 1, :]
        fwide[i] = jnp.broadcast_to(line * TIME_STEP, (TILE, lon))

    def advance(u, upper, lower, force):
        eastern = pltpu.roll(u, lon - 1, 1)
        western = pltpu.roll(u, 1, 1)
        far_west = pltpu.roll(u, 2, 1)
        tendency = (eastern - far_west) * western - u + LAT_MIXING * (upper + lower - 2.0 * u)
        return u + (TIME_STEP * tendency + force)

    def forecast(start):
        span = pl.ds(pl.multiple_of(start, TILE), TILE)
        state = [ext[i, span, :] for i in range(2 * STEPS + rows)]
        for step in range(STEPS):
            lo = step + 1
            fresh = []
            for i in range(lo, 2 * STEPS + rows - lo):
                at = i - step
                moved = advance(state[at], state[at + 1], state[at - 1], fwide[i])
                if i < STEPS:
                    moved = jnp.where(has_before, moved, 0.0)
                elif i >= STEPS + rows:
                    moved = jnp.where(has_after, moved, 0.0)
                fresh.append(moved)
            state = fresh
        for r in range(rows):
            cur[r, span, :] = state[r]

    for c in range(HALO_CHUNKS):
        for side in range(2):
            @pl.when(can_receive[side])
            def _(side=side, c=c):
                halo_copy(side, c).wait_recv()

        @pl.loop(0, chunk // TILE)
        def _(i, c=c):
            forecast(c * chunk + i * TILE)

    def gram_copy(d):
        target = lax.rem(me + d, n_mem)
        return pltpu.make_async_remote_copy(
            src_ref=gsend.at[target // share],
            dst_ref=grecv.at[d - 1],
            send_sem=gram_send.at[d - 1],
            recv_sem=gram_recv.at[d - 1],
            device_id={"mem": target},
            device_id_type=MESH,
        )

    def moments(row):
        values = cur[row]
        mean = jnp.sum(values, axis=0, keepdims=True) * (1.0 / members)
        high, low = split(values - mean)
        square = lax.dot_general(
            jnp.concatenate([high, high, low], axis=0), jnp.concatenate([high, low, high], axis=0),
            (((0,), (0,)), ((), ())), preferred_element_type=jnp.float32,
        )
        gsend[row, 0:PATCH_CELLS, :] = diagonal_blocks(square)
        gsend[row, PATCH_CELLS:, :] = jnp.broadcast_to(mean, (TILE, lon))

    @pl.loop(1, n_mem)
    def _(d):
        target = lax.rem(me + d, n_mem)

        @pl.when(lax.rem(target, share) == 0)
        def _():
            moments(target // share)
            gram_copy(d).start()

    def gain_copy(d):
        return pltpu.make_async_remote_copy(
            src_ref=nsend,
            dst_ref=nrecv.at[my_row],
            send_sem=gain_send.at[d - 1],
            recv_sem=gain_recv.at[d - 1],
            device_id={"mem": lax.rem(me + d, n_mem)},
            device_id_type=MESH,
        )

    def apply(row, gain_ref):
        mean = gain_ref[PATCH_CELLS:PATCH_CELLS + 1, :]
        shift = gain_ref[PATCH_CELLS + 1:PATCH_CELLS + 2, :]
        half = 0.5 * (cur[row] - mean)
        high, low = split(half)
        gain_high, gain_low = (
            block_diagonal(part.astype(jnp.float32)).astype(jnp.bfloat16)
            for part in split(gain_ref[0:PATCH_CELLS, :])
        )
        moved = (
            jnp.dot(high, gain_high, preferred_element_type=jnp.float32)
            + jnp.dot(high, gain_low, preferred_element_type=jnp.float32)
            + jnp.dot(low, gain_high, preferred_element_type=jnp.float32)
        )
        result = half + moved + (mean + shift)
        for h in range(lon // 128):
            out_ref[pl.ds(h * rows + row, members, stride=rows * (lon // 128)), :] = result[:, h * 128:(h + 1) * 128]

    @pl.when(solver)
    def _():
        moments(my_row)
        total = gsend[my_row, 0:PATCH_CELLS, :]
        means = [gsend[my_row, PATCH_CELLS:, :]]
        for d in range(1, n_mem):
            gram_copy(d).wait_recv()
            total = total + grecv[d - 1, 0:PATCH_CELLS, :]
            means.append(grecv[d - 1, PATCH_CELLS:, :])
        mean = functools.reduce(lambda a, b: a + b, means)[0:1] * (1.0 / n_mem)
        drift = jnp.concatenate([m[0:1] - mean for m in means], axis=0)
        spread = lax.dot_general(
            drift, drift, (((0,), (0,)), ((), ())), precision=HIGHEST, preferred_element_type=jnp.float32
        )
        cov = (total + members * diagonal_blocks(spread)) * (1.0 / (members * n_mem - 1))

        in_group = lax.broadcasted_iota(jnp.int32, (PATCH_CELLS, lon), 1) - groups * PATCH_CELLS
        eye = lax.broadcasted_iota(jnp.int32, (PATCH_CELLS, lon), 0) == in_group
        inverse = invert(jnp.where(eye, 1.0, 0.0) + weight * cov)
        misfit = pull - weight * as_column(mean, eye, groups)
        push = jnp.sum(misfit * cov, axis=0, keepdims=True)
        shift = jnp.sum(as_column(push, eye, groups) * inverse, axis=0, keepdims=True)
        nsend[0:PATCH_CELLS, :] = inverse
        first = lax.broadcasted_iota(jnp.int32, (TILE, lon), 0) == 0
        nsend[PATCH_CELLS:, :] = jnp.where(first, mean, shift)
        for d in range(1, n_mem):
            gain_copy(d).start()
        apply(my_row, nsend)

    @pl.loop(1, n_mem)
    def _(d):
        origin = lax.rem(me + n_mem - d, n_mem)

        @pl.when(lax.rem(origin, share) == 0)
        def _():
            gain_copy(d).wait_recv()
            apply(origin // share, nrecv.at[origin // share])

    for side in range(2):
        @pl.when(can_send[side])
        def _(side=side):
            force_copy(side).wait_send()
            for c in range(HALO_CHUNKS):
                halo_copy(side, c).wait_send()

    @pl.loop(1, n_mem)
    def _(d):
        @pl.when(lax.rem(lax.rem(me + d, n_mem), share) == 0)
        def _():
            gram_copy(d).wait_send()

        @pl.when(solver)
        def _():
            gain_copy(d).wait_send()


def local(n_mem, n_lat, fields, forcing, obs_cell, obs_count, obs_value, obs_var):
    members, rows, lon = fields.shape
    slots = obs_cell.shape[2]
    per_row = lon // PATCH_CELLS
    if obs_count.shape[1] != per_row:
        row = lax.axis_index("mem") // (n_mem // rows)
        obs_count, obs_value, obs_var = (
            lax.dynamic_slice_in_dim(lax.all_gather(a, "mem", axis=1, tiled=True), row * per_row, per_row, 1)
            for a in (obs_count, obs_value, obs_var)
        )
    block = PATCH_CELLS + TILE
    vmem = pl.BlockSpec(memory_space=pltpu.VMEM)
    dma = pltpu.SemaphoreType.DMA
    out = pl.pallas_call(
        functools.partial(kernel, n_mem, n_lat),
        out_shape=jax.ShapeDtypeStruct((members * rows * (lon // 128), 128), jnp.float32),
        in_specs=[pl.BlockSpec(memory_space=pl.ANY), vmem, vmem, pl.BlockSpec(memory_space=pltpu.SMEM), vmem, vmem],
        out_specs=vmem,
        scratch_shapes=[
            pltpu.VMEM((members * rows * (lon // 128), 128), jnp.float32),
            pltpu.VMEM((rows + 2 * STEPS, members, lon), jnp.float32),
            pltpu.VMEM((rows, members, lon), jnp.float32),
            pltpu.VMEM((2, rows, lon), jnp.float32),
            pltpu.VMEM((rows + 2 * STEPS, TILE, lon), jnp.float32),
            pltpu.VMEM((rows, block, lon), jnp.float32),
            pltpu.VMEM((n_mem - 1, block, lon), jnp.float32),
            pltpu.VMEM((block, lon), jnp.float32),
            pltpu.VMEM((rows, block, lon), jnp.float32),
            dma((HALO_CHUNKS,)),
            dma((2, HALO_CHUNKS)), dma((2, HALO_CHUNKS)),
            dma((2,)), dma((2,)),
            dma((n_mem - 1,)), dma((n_mem - 1,)),
            dma((n_mem - 1,)), dma((n_mem - 1,)),
        ],
        compiler_params=pltpu.CompilerParams(collective_id=0, has_side_effects=True),
        name="cycle",
    )(
        fields.reshape(members, rows, lon // 128, 128).transpose(0, 2, 1, 3).reshape(-1, 128),
        forcing,
        obs_cell.reshape(-1, slots),
        obs_count,
        obs_value.reshape(-1, slots),
        obs_var.reshape(-1, slots),
    )
    return out.reshape(members, lon // 128, rows, 128).transpose(0, 2, 1, 3).reshape(members, rows, lon)


def solution(mesh):
    placed = (
        P("mem", "lat", None),
        P("lat", None),
        P("lat", None, None),
        P("lat", "mem"),
        P("lat", "mem", None),
        P("lat", "mem", None),
    )
    return jax.shard_map(
        functools.partial(local, mesh.shape["mem"], mesh.shape["lat"]),
        mesh=mesh, in_specs=placed, out_specs=P("mem", "lat", None), check_vma=False,
    )
```

```python
import functools

import jax
import jax.numpy as jnp
from jax import lax
from jax.experimental import pallas as pl
from jax.experimental.pallas import tpu as pltpu
from jax.sharding import PartitionSpec as P

PATCH_CELLS = 64
STEPS = 4
TIME_STEP = 0.05
LAT_MIXING = 4.0
HALO_CHUNKS = 8
TILE = 8
PIVOTS = 4

MESH = pl.DeviceIdType.MESH
HIGHEST = lax.Precision.HIGHEST


def lane_group(shape):
    return lax.broadcasted_iota(jnp.int32, shape, 1) // PATCH_CELLS


def diagonal_blocks(square):
    lon = square.shape[1]
    groups = lane_group((PATCH_CELLS, lon))
    total = jnp.zeros((PATCH_CELLS, lon), jnp.float32)
    for q in range(lon // PATCH_CELLS):
        block = square[q * PATCH_CELLS:(q + 1) * PATCH_CELLS]
        total = jnp.where(groups == q, block, total)
    return total


def block_diagonal(blocks):
    lon = blocks.shape[1]
    groups = lane_group(blocks.shape)
    return jnp.concatenate(
        [jnp.where(groups == q, blocks, 0.0) for q in range(lon // PATCH_CELLS)], axis=0
    )


def as_column(row, eye, groups):
    spread = jnp.where(eye, jnp.broadcast_to(row, eye.shape), 0.0)
    total = jnp.zeros(eye.shape, jnp.float32)
    for q in range(eye.shape[1] // PATCH_CELLS):
        column = jnp.sum(jnp.where(groups == q, spread, 0.0), axis=1, keepdims=True)
        total = jnp.where(groups == q, column, total)
    return total


def invert(blocks):
    lon = blocks.shape[1]
    sublane = lax.broadcasted_iota(jnp.int32, (PATCH_CELLS, 128), 0)
    lane = lax.broadcasted_iota(jnp.int32, (PATCH_CELLS, 128), 1)
    start = (lane // PATCH_CELLS) * PATCH_CELLS
    position = lane - start
    halves = [blocks[:, h * 128:(h + 1) * 128] for h in range(lon // 128)]
    span = range(PIVOTS)
    for k in range(0, PATCH_CELLS, PIVOTS):
        in_columns = (position >= k) & (position < k + PIVOTS)
        in_rows = (sublane >= k) & (sublane < k + PIVOTS)
        updated = []
        for half in halves:
            columns = [
                jnp.take_along_axis(half, start + (k + j), axis=1, mode="promise_in_bounds") for j in span
            ]
            small = [[columns[j][k + i:k + i + 1] for j in span] for i in span]
            rows = [
                jnp.where(
                    in_columns[0:1],
                    jnp.where(position[0:1] == k + i, 1.0, 0.0),
                    half[k + i:k + i + 1],
                )
                for i in span
            ]
            for i in span:
                inverse = 1.0 / small[i][i]
                rows[i] = rows[i] * inverse
                for j in range(i + 1, PIVOTS):
                    small[i][j] = small[i][j] * inverse
                for other in span:
                    if other != i:
                        factor = small[other][i]
                        rows[other] = rows[other] - factor * rows[i]
                        for j in range(i + 1, PIVOTS):
                            small[other][j] = small[other][j] - factor * small[i][j]
            fresh = jnp.where(in_columns | in_rows, 0.0, half)
            for j in span:
                factor = jnp.where(in_rows, jnp.where(sublane == k + j, -1.0, 0.0), columns[j])
                fresh = fresh - factor * rows[j]
            updated.append(fresh)
        halves = updated
    return jnp.concatenate(halves, axis=1)


def split(values):
    high = values.astype(jnp.bfloat16)
    return high, (values - high.astype(jnp.float32)).astype(jnp.bfloat16)


def kernel(n_mem, n_lat, fields_ref, forcing_in, cell_in, count_in, value_in, var_in, out_ref,
           forcing_ref, cell_ref, count_ref, value_ref, var_ref, landed, ext, cur, fbuf, fwide, gsend, grecv, nsend, nrecv,
           small_sem, load_sem, halo_send, halo_recv, force_send, force_recv, gram_send, gram_recv, gain_send, gain_recv):
    rows, members, lon = cur.shape
    share = n_mem // rows
    per_row = lon // PATCH_CELLS
    chunk = members // HALO_CHUNKS
    me = lax.axis_index("mem")
    strip = lax.axis_index("lat")
    has_before = strip > 0
    has_after = strip < n_lat - 1
    my_row = me // share
    solver = lax.rem(me, share) == 0

    barrier = pltpu.get_barrier_semaphore()
    for d in range(1, n_mem):
        pl.semaphore_signal(barrier, inc=1, device_id={"mem": lax.rem(me + d, n_mem)}, device_id_type=MESH)

    @pl.when(has_before)
    def _():
        pl.semaphore_signal(barrier, inc=1, device_id={"lat": strip - 1}, device_id_type=MESH)

    @pl.when(has_after)
    def _():
        pl.semaphore_signal(barrier, inc=1, device_id={"lat": strip + 1}, device_id_type=MESH)

    small = [
        pltpu.make_async_copy(source, target, small_sem.at[i])
        for i, (source, target) in enumerate((
            (forcing_in, forcing_ref), (cell_in, cell_ref), (count_in, count_ref),
            (value_in, value_ref), (var_in, var_ref),
        ))
    ]
    for copy in small:
        copy.start()
    pitch = rows * (lon // 128)

    def load(c):
        span = pl.ds(c * chunk * pitch, chunk * pitch)
        return pltpu.make_async_copy(fields_ref.at[span], landed.at[span], load_sem.at[c])

    for c in range(HALO_CHUNKS):
        load(c).start()

    def rows_first(c):
        load(c).wait()
        for r in range(rows):
            for h in range(lon // 128):
                ext[STEPS + r, c * chunk:(c + 1) * chunk, h * 128:(h + 1) * 128] = landed[
                    pl.ds(c * chunk * pitch + h * rows + r, chunk, stride=pitch), :]

    rows_first(0)
    for copy in small:
        copy.wait()
    pl.semaphore_wait(barrier, n_mem - 1 + has_before.astype(jnp.int32) + has_after.astype(jnp.int32))

    def halo_copy(side, c):
        span = pl.ds(c * chunk, chunk)
        source, target = ((rows, 0), (STEPS, STEPS + rows))[side]
        return pltpu.make_async_remote_copy(
            src_ref=ext.at[pl.ds(source, STEPS), span],
            dst_ref=ext.at[pl.ds(target, STEPS), span],
            send_sem=halo_send.at[side, c],
            recv_sem=halo_recv.at[side, c],
            device_id={"lat": (strip + 1, strip - 1)[side]},
            device_id_type=MESH,
        )

    def force_copy(side):
        return pltpu.make_async_remote_copy(
            src_ref=forcing_ref,
            dst_ref=fbuf.at[side],
            send_sem=force_send.at[side],
            recv_sem=force_recv.at[side],
            device_id={"lat": (strip + 1, strip - 1)[side]},
            device_id_type=MESH,
        )

    can_send = (has_after, has_before)
    can_receive = (has_before, has_after)
    for side in range(2):
        @pl.when(can_send[side])
        def _(side=side):
            force_copy(side).start()
    for c in range(HALO_CHUNKS):
        if c:
            rows_first(c)
        for side in range(2):
            @pl.when(can_send[side])
            def _(side=side, c=c):
                halo_copy(side, c).start()

    @pl.when(jnp.logical_not(has_before))
    def _():
        ext[0:STEPS] = jnp.zeros((STEPS, members, lon), jnp.float32)
        fbuf[0] = jnp.zeros((rows, lon), jnp.float32)

    @pl.when(jnp.logical_not(has_after))
    def _():
        ext[STEPS + rows:] = jnp.zeros((STEPS, members, lon), jnp.float32)
        fbuf[1] = jnp.zeros((rows, lon), jnp.float32)

    cell_of = lax.broadcasted_iota(jnp.int32, (PATCH_CELLS, cell_ref.shape[1]), 0)
    slot = lax.broadcasted_iota(jnp.int32, (1, cell_ref.shape[1]), 1)
    groups = lane_group((PATCH_CELLS, lon))
    weight = jnp.zeros((PATCH_CELLS, lon), jnp.float32)
    pull = jnp.zeros((PATCH_CELLS, lon), jnp.float32)
    for q in range(per_row):
        cells = cell_ref[pl.ds(my_row * per_row + q, 1), :]
        precision = jnp.where(slot < count_ref[0, q], 1.0 / var_ref[q:q + 1, :], 0.0)
        hit = cell_of == cells
        w = jnp.sum(jnp.where(hit, precision, 0.0), axis=1, keepdims=True)
        b = jnp.sum(jnp.where(hit, precision * value_ref[q:q + 1, :], 0.0), axis=1, keepdims=True)
        weight = jnp.where(groups == q, w, weight)
        pull = jnp.where(groups == q, b, pull)

    for side in range(2):
        @pl.when(can_receive[side])
        def _(side=side):
            force_copy(side).wait_recv()
    own = forcing_ref[...]
    for i in range(2 * STEPS + rows):
        if i < STEPS:
            line = fbuf[0, rows - STEPS + i:rows - STEPS + i + 1, :]
        elif i < STEPS + rows:
            line = own[i - STEPS:i - STEPS + 1]
        else:
            line = fbuf[1, i - STEPS - rows:i - STEPS - rows + 1, :]
        fwide[i] = jnp.broadcast_to(line * TIME_STEP, (TILE, lon))

    def advance(u, upper, lower, force):
        eastern = pltpu.roll(u, lon - 1, 1)
        western = pltpu.roll(u, 1, 1)
        far_west = pltpu.roll(u, 2, 1)
        tendency = (eastern - far_west) * western - u + LAT_MIXING * (upper + lower - 2.0 * u)
        return u + (TIME_STEP * tendency + force)

    def forecast(start):
        span = pl.ds(pl.multiple_of(start, TILE), TILE)
        state = [ext[i, span, :] for i in range(2 * STEPS + rows)]
        for step in range(STEPS):
            lo = step + 1
            fresh = []
            for i in range(lo, 2 * STEPS + rows - lo):
                at = i - step
                moved = advance(state[at], state[at + 1], state[at - 1], fwide[i])
                if i < STEPS:
                    moved = jnp.where(has_before, moved, 0.0)
                elif i >= STEPS + rows:
                    moved = jnp.where(has_after, moved, 0.0)
                fresh.append(moved)
            state = fresh
        for r in range(rows):
            cur[r, span, :] = state[r]

    for c in range(HALO_CHUNKS):
        for side in range(2):
            @pl.when(can_receive[side])
            def _(side=side, c=c):
                halo_copy(side, c).wait_recv()

        @pl.loop(0, chunk // TILE)
        def _(i, c=c):
            forecast(c * chunk + i * TILE)

    def gram_copy(d):
        target = lax.rem(me + d, n_mem)
        return pltpu.make_async_remote_copy(
            src_ref=gsend.at[target // share],
            dst_ref=grecv.at[d - 1],
            send_sem=gram_send.at[d - 1],
            recv_sem=gram_recv.at[d - 1],
            device_id={"mem": target},
            device_id_type=MESH,
        )

    def moments(row):
        values = cur[row]
        mean = jnp.sum(values, axis=0, keepdims=True) * (1.0 / members)
        high, low = split(values - mean)
        square = lax.dot_general(
            jnp.concatenate([high, high, low], axis=0), jnp.concatenate([high, low, high], axis=0),
            (((0,), (0,)), ((), ())), preferred_element_type=jnp.float32,
        )
        gsend[row, 0:PATCH_CELLS, :] = diagonal_blocks(square)
        gsend[row, PATCH_CELLS:, :] = jnp.broadcast_to(mean, (TILE, lon))

    @pl.loop(1, n_mem)
    def _(d):
        target = lax.rem(me + d, n_mem)

        @pl.when(lax.rem(target, share) == 0)
        def _():
            moments(target // share)
            gram_copy(d).start()

    def gain_copy(d):
        return pltpu.make_async_remote_copy(
            src_ref=nsend,
            dst_ref=nrecv.at[my_row],
            send_sem=gain_send.at[d - 1],
            recv_sem=gain_recv.at[d - 1],
            device_id={"mem": lax.rem(me + d, n_mem)},
            device_id_type=MESH,
        )

    def apply(row, gain_ref):
        mean = gain_ref[PATCH_CELLS:PATCH_CELLS + 1, :]
        shift = gain_ref[PATCH_CELLS + 1:PATCH_CELLS + 2, :]
        half = 0.5 * (cur[row] - mean)
        high, low = split(half)
        gain_high, gain_low = (
            block_diagonal(part.astype(jnp.float32)).astype(jnp.bfloat16)
            for part in split(gain_ref[0:PATCH_CELLS, :])
        )
        moved = (
            jnp.dot(high, gain_high, preferred_element_type=jnp.float32)
            + jnp.dot(high, gain_low, preferred_element_type=jnp.float32)
            + jnp.dot(low, gain_high, preferred_element_type=jnp.float32)
        )
        result = half + moved + (mean + shift)
        for h in range(lon // 128):
            out_ref[pl.ds(h * rows + row, members, stride=rows * (lon // 128)), :] = result[:, h * 128:(h + 1) * 128]

    @pl.when(solver)
    def _():
        moments(my_row)
        total = gsend[my_row, 0:PATCH_CELLS, :]
        means = [gsend[my_row, PATCH_CELLS:, :]]
        for d in range(1, n_mem):
            gram_copy(d).wait_recv()
            total = total + grecv[d - 1, 0:PATCH_CELLS, :]
            means.append(grecv[d - 1, PATCH_CELLS:, :])
        mean = functools.reduce(lambda a, b: a + b, means)[0:1] * (1.0 / n_mem)
        drift = jnp.concatenate([m[0:1] - mean for m in means], axis=0)
        spread = lax.dot_general(
            drift, drift, (((0,), (0,)), ((), ())), precision=HIGHEST, preferred_element_type=jnp.float32
        )
        cov = (total + members * diagonal_blocks(spread)) * (1.0 / (members * n_mem - 1))

        in_group = lax.broadcasted_iota(jnp.int32, (PATCH_CELLS, lon), 1) - groups * PATCH_CELLS
        eye = lax.broadcasted_iota(jnp.int32, (PATCH_CELLS, lon), 0) == in_group
        inverse = invert(jnp.where(eye, 1.0, 0.0) + weight * cov)
        misfit = pull - weight * as_column(mean, eye, groups)
        push = jnp.sum(misfit * cov, axis=0, keepdims=True)
        shift = jnp.sum(as_column(push, eye, groups) * inverse, axis=0, keepdims=True)
        nsend[0:PATCH_CELLS, :] = inverse
        first = lax.broadcasted_iota(jnp.int32, (TILE, lon), 0) == 0
        nsend[PATCH_CELLS:, :] = jnp.where(first, mean, shift)
        for d in range(1, n_mem):
            gain_copy(d).start()
        apply(my_row, nsend)

    @pl.loop(1, n_mem)
    def _(d):
        origin = lax.rem(me + n_mem - d, n_mem)

        @pl.when(lax.rem(origin, share) == 0)
        def _():
            gain_copy(d).wait_recv()
            apply(origin // share, nrecv.at[origin // share])

    for side in range(2):
        @pl.when(can_send[side])
        def _(side=side):
            force_copy(side).wait_send()
            for c in range(HALO_CHUNKS):
                halo_copy(side, c).wait_send()

    @pl.loop(1, n_mem)
    def _(d):
        @pl.when(lax.rem(lax.rem(me + d, n_mem), share) == 0)
        def _():
            gram_copy(d).wait_send()

        @pl.when(solver)
        def _():
            gain_copy(d).wait_send()


def local(n_mem, n_lat, fields, forcing, obs_cell, obs_count, obs_value, obs_var):
    members, rows, lon = fields.shape
    slots = obs_cell.shape[2]
    per_row = lon // PATCH_CELLS
    if obs_count.shape[1] != per_row:
        row = lax.axis_index("mem") // (n_mem // rows)
        obs_count, obs_value, obs_var = (
            lax.dynamic_slice_in_dim(lax.all_gather(a, "mem", axis=1, tiled=True), row * per_row, per_row, 1)
            for a in (obs_count, obs_value, obs_var)
        )
    block = PATCH_CELLS + TILE
    vmem = pl.BlockSpec(memory_space=pltpu.VMEM)
    dma = pltpu.SemaphoreType.DMA
    out = pl.pallas_call(
        functools.partial(kernel, n_mem, n_lat),
        out_shape=jax.ShapeDtypeStruct((members * rows * (lon // 128), 128), jnp.float32),
        in_specs=[pl.BlockSpec(memory_space=pltpu.HBM)] * 6,
        out_specs=vmem,
        scratch_shapes=[
            pltpu.VMEM(forcing.shape, jnp.float32),
            pltpu.VMEM((obs_cell.shape[1], slots), jnp.int32),
            pltpu.SMEM(obs_count.shape, jnp.int32),
            pltpu.VMEM((per_row, slots), jnp.float32),
            pltpu.VMEM((per_row, slots), jnp.float32),
            pltpu.VMEM((members * rows * (lon // 128), 128), jnp.float32),
            pltpu.VMEM((rows + 2 * STEPS, members, lon), jnp.float32),
            pltpu.VMEM((rows, members, lon), jnp.float32),
            pltpu.VMEM((2, rows, lon), jnp.float32),
            pltpu.VMEM((rows + 2 * STEPS, TILE, lon), jnp.float32),
            pltpu.VMEM((rows, block, lon), jnp.float32),
            pltpu.VMEM((n_mem - 1, block, lon), jnp.float32),
            pltpu.VMEM((block, lon), jnp.float32),
            pltpu.VMEM((rows, block, lon), jnp.float32),
            dma((5,)),
            dma((HALO_CHUNKS,)),
            dma((2, HALO_CHUNKS)), dma((2, HALO_CHUNKS)),
            dma((2,)), dma((2,)),
            dma((n_mem - 1,)), dma((n_mem - 1,)),
            dma((n_mem - 1,)), dma((n_mem - 1,)),
        ],
        compiler_params=pltpu.CompilerParams(collective_id=0, has_side_effects=True, vmem_limit_bytes=16 * 2 ** 20),
        name="cycle",
    )(*(pltpu.with_memory_space_constraint(a, pltpu.HBM) for a in (
        fields.reshape(members, rows, lon // 128, 128).transpose(0, 2, 1, 3).reshape(-1, 128),
        forcing,
        obs_cell.reshape(-1, slots),
        obs_count,
        obs_value.reshape(-1, slots),
        obs_var.reshape(-1, slots),
    )))
    return out.reshape(members, lon // 128, rows, 128).transpose(0, 2, 1, 3).reshape(members, rows, lon)


def solution(mesh):
    placed = (
        P("mem", "lat", None),
        P("lat", None),
        P("lat", None, None),
        P("lat", "mem"),
        P("lat", "mem", None),
        P("lat", "mem", None),
    )
    return jax.shard_map(
        functools.partial(local, mesh.shape["mem"], mesh.shape["lat"]),
        mesh=mesh, in_specs=placed, out_specs=P("mem", "lat", None), check_vma=False,
    )
```
